512 devices in a mesh: grp: 16 (over y_hi, x), pen: 32 (over y_lo, z, core).
Axes of the slice: x: 4, y: 8 (y_hi: 4, y_lo: 2; y = y_hi * 2 + y_lo), z: 8, core: 2. Of those that a mesh axis runs over, the one named last changes fastest.
Arguments:
- flow_fields: float32 [4, 16, 1536, 1536], P(None, 'grp', 'pen'), may hold values from -6 to 6
- marker_cells: int32 [16, 32, 1024, 8], P('grp', 'pen'), may hold values from 0 to 73727
- marker_weights: float32 [16, 32, 1024, 8], P('grp', 'pen'), may hold values from 0.05 to 0.3
- solid_blocks: int32 [16, 1536, 12], P('grp', 'pen'), may hold values 0 or 1
Outputs:
- velocity_next: float32 [3, 16, 1536, 1536], P(None, 'grp', 'pen')
- poisson_source: float32 [16, 1536, 1536], P(None, 'pen', 'grp')
The draws below stay inside these ranges and needn't reach their ends.
Inputs may be any that keep to these rules, and one draw needn't show every extreme that they name: `marker_cells`: each entry numbers a cell of the device's own home block of 73728 cells, first dimension slowest, third fastest.
All inputs are finite; a program needn't handle non-finite values. No bound on the sum of `solid_blocks` on one device may be relied on, other than what follows from the above.
Results may differ from the reference program's by a relative error of at most 0.0003.
Values sent between devices are 32-bit elements; how exact they have to be, the bound alone decides.
A program may use at most 128 MiB of HBM per device.

```python
import math
import jax
import jax.numpy as jnp
from jax import lax

NY = 1536
NZ = 1536
CX = 1
MK = 1024
STEN = 8
ZB = 128
NX = 16
CELLS = 73728
N_GRP = 16
N_PEN = 32


def plant(entries, rng, smallest, top_value):
    longest = entries.shape.index(max(entries.shape))
    spots = []
    for shift in (0, 1):
        where = [jax.random.randint(jax.random.fold_in(rng, axis), (), 0, length) for axis, length in enumerate(entries.shape)]
        where[longest] = (where[longest] + shift) % entries.shape[longest]
        spots.append(tuple(where))
    return entries.at[spots[0]].set(smallest).at[spots[1]].set(top_value)


def block_scale(own_key, shape, split, least, largest):
    level, own = 1.0, jax.random.fold_in(own_key, 6)
    for position, shards_of in split:
        steps = jnp.exp(jax.random.uniform(jax.random.fold_in(own, position), (shards_of,), jnp.float32, least / len(split), largest / len(split)))
        level = level * jnp.repeat(steps, shape[position] // shards_of).reshape([-1 if axis == position else 1 for axis in range(len(shape))])
    return level


def bell_draw(rng, extent, scale, limit, split=(), kind=jnp.bfloat16):
    result = scale * jax.random.normal(rng, extent, jnp.float32)
    if split:
        result = result * block_scale(rng, extent, split, -0.22, 0.18)
    return jnp.clip(result, -limit, limit).astype(kind)


def setup_inputs(seed: int = 0) -> dict:
    key_of = jax.random.split(jax.random.key(seed), 5)
    return {
        "flow_fields": bell_draw(key_of[0], (4, NX, NY, NZ), 1.0, 6.0, ((1, 16), (2, 32)), jnp.float32),
        "marker_cells": plant(jax.random.randint(key_of[1], (N_GRP, N_PEN, MK, STEN), 0, CELLS), jax.random.fold_in(key_of[1], 1), 0, CELLS - 1).astype(jnp.int32),
        "marker_weights": jnp.clip(0.05 + 0.25 * jax.random.uniform(key_of[2], (N_GRP, N_PEN, MK, STEN), jnp.float32) ** block_scale(key_of[2], (N_GRP, N_PEN, MK, STEN), ((0, 16), (1, 32)), -0.2, 0.2), 0.05, 0.3),
        "solid_blocks": plant((jax.random.randint(key_of[3], (NX, NY, NZ // ZB), 0, 8) < 1).astype(jnp.int32), jax.random.fold_in(key_of[3], 1), 0, 1),
    }


def compact(line_data):
    length = line_data.shape[0]
    padded = jnp.pad(line_data, ((2, 2), (0, 0)))
    source = 14.0 / 9.0 * 0.5 * (padded[3:-1] - padded[1:-3]) + 1.0 / 9.0 * 0.25 * (padded[4:] - padded[:-4])
    lower_band = jnp.full((length,), 1.0 / 3.0, dtype=line_data.dtype).at[0].set(0.0)
    upper_band = jnp.full((length,), 1.0 / 3.0, dtype=line_data.dtype).at[length - 1].set(0.0)
    middle_band = jnp.ones((length,), dtype=line_data.dtype)
    return lax.linalg.tridiagonal_solve(lower_band, middle_band, upper_band, source)

def spectral(field, axis):
    length = field.shape[axis]
    spectrum = jnp.fft.rfft(field, axis=axis)
    mode_index = jnp.arange(length // 2 + 1).astype(field.dtype)
    wavenumber = jnp.where(mode_index < length // 2, 2.0 * math.pi / length * mode_index, 0.0).astype(field.dtype)
    shape_list = [1] * field.ndim
    shape_list[axis] = length // 2 + 1
    factor = wavenumber.reshape(shape_list)
    derived = jnp.fft.irfft(spectrum * (1j * factor), n=length, axis=axis)
    return derived.astype(field.dtype)

def along_axis(field, axis):
    if axis == 0:
        shaped = field.shape
        return compact(field.reshape(shaped[0], -1)).reshape(shaped)
    return spectral(field, axis)

def reference(flow_fields, marker_cells, marker_weights, solid_blocks):
    velocity = flow_fields[:3]
    pressure = flow_fields[3]
    tendency = [jnp.zeros_like(pressure) for _ in range(3)]
    divergence = jnp.zeros_like(pressure)
    for direction in range(3):
        for component in range(3):
            slope = along_axis(velocity[component], direction)
            tendency[component] = tendency[component] - velocity[direction] * slope
            if component == direction:
                divergence = divergence + slope
        tendency[direction] = tendency[direction] - along_axis(pressure, direction)
    provisional = velocity + 0.1 * jnp.stack(tendency)
    cyl = NY // N_PEN
    blocks = N_GRP * N_PEN
    blocked = provisional.reshape(3, N_GRP, CX, N_PEN, cyl, NZ).transpose(0, 1, 3, 2, 4, 5).reshape(3, blocks, CELLS)
    cells_index = marker_cells.reshape(blocks, MK * STEN).astype(jnp.int32)
    weights = marker_weights.reshape(blocks, MK, STEN)
    gathered = jnp.take_along_axis(blocked, cells_index[None], axis=2).reshape(3, blocks, MK, STEN)
    sampled = jnp.sum(gathered * weights[None], axis=3)
    spread = (sampled[..., None] * weights[None]).reshape(3, blocks * MK * STEN)
    offsets = (jnp.arange(blocks, dtype=jnp.int32) * CELLS)[:, None]
    global_index = (cells_index + offsets).reshape(-1)
    correction = jnp.zeros((3, blocks * CELLS), provisional.dtype).at[:, global_index].add(spread)
    correction = correction.reshape(3, N_GRP, N_PEN, CX, cyl, NZ).transpose(0, 1, 3, 2, 4, 5).reshape(3, NX, NY, NZ)
    solid = jnp.repeat(solid_blocks, ZB, axis=2).astype(provisional.dtype)
    velocity_next = (1.0 - solid)[None] * (provisional - correction)
    return (velocity_next, divergence)
```

```python
import math

import jax
import jax.numpy as jnp
import numpy as np
from jax import lax
from jax.experimental import pallas as pl
from jax.experimental.pallas import tpu as pltpu
from jax.sharding import PartitionSpec as P

MESH = pl.DeviceIdType.MESH
F32, BF16 = jnp.float32, jnp.bfloat16
NG, NP = 16, 32
ROWS, NZ, HALF = 48, 1536, 768
LANES, SPLIT, MK, ST = 128, 512, 1024, 8
PACK = ROWS + ROWS // 2


def bf16_parts(values):
    high = values.astype(BF16)
    return high, (values - high.astype(F32)).astype(BF16)


def table_rows():
    lag = np.arange(2 * HALF)
    safe = np.where(lag % HALF == 0, 1, lag)
    line = math.pi / NZ * (1 - 2 * (lag % 2)) / np.tan(math.pi * safe / NZ)
    line = np.where(lag % HALF == 0, 0.0, line)
    other = np.roll(line, -HALF)
    rows = []
    for values, width in ((0.5 * (line + other), HALF), (0.5 * (line - other), 2 * HALF)):
        where = (np.arange(16)[:, None] - np.arange(width)[None, :]) % (2 * HALF)
        block = values[where].astype(np.float32)
        high = block.astype(jnp.bfloat16).astype(np.float32)
        rows += [high, (block - high).astype(jnp.bfloat16).astype(np.float32)]
    return rows


def elimination():
    upper, scale, last = [], [], 0.0
    for _ in range(NG):
        pivot = 1.0 / (1.0 - last / 3.0)
        last = pivot / 3.0
        upper.append(last)
        scale.append(pivot)
    return upper, scale


def kernel(
    flow, cells, weights, solid, rah, ral, rbh, rbl,
    vel, pois,
    psend, precv, pmid, pback, grecv, gmid, gback, dsend, drecv,
    tah, tal, tbh, tbl, xsh, xsl, xdh, xdl, ysum, ydif, fsh, fsl, fdh, fdl,
    pre, div, prov, phi, plo, hot, corr, acc,
    ssem, rsem,
):
    me_g, me_p = lax.axis_index("grp"), lax.axis_index("pen")
    lane = lax.broadcasted_iota(jnp.int32, (ROWS // 2, LANES), 1) < LANES // 2
    dot = lambda a, b: jnp.dot(a, b, preferred_element_type=F32)

    barrier = pltpu.get_barrier_semaphore()

    def greet(axis, me, count):
        def step(d, carry):
            pl.semaphore_signal(
                barrier, 1, device_id={axis: lax.rem(me + d, count)}, device_id_type=MESH
            )
            return carry
        lax.fori_loop(1, count, step, 0)

    greet("pen", me_p, NP)
    greet("grp", me_g, NG)

    def push(axis, me, count, source, target, phase, whole=True):
        def step(d, carry):
            peer = lax.rem(me + d, count)
            if whole:
                src = source.at[peer]
            else:
                start = pl.multiple_of(lax.rem(peer, 4) * 384, 128)
                src = source.at[lax.div(peer, 4), :, pl.ds(start, 384)]
            pltpu.make_async_remote_copy(
                src_ref=src, dst_ref=target.at[me],
                send_sem=ssem.at[phase], recv_sem=rsem.at[phase],
                device_id={axis: peer}, device_id_type=MESH,
            ).start()
            return carry
        lax.fori_loop(1, count, step, 0)

    def arrived(target, count, phase):
        ref = target.at[pl.ds(0, count - 1)]
        pltpu.make_async_copy(ref, ref, rsem.at[phase]).wait()

    def sent(source, count, phase):
        ref = source.at[pl.ds(0, count - 1)]
        pltpu.make_async_copy(ref, ref, ssem.at[phase]).wait()

    for tile in range(NP):
        psend[tile, :ROWS, :] = flow[tile // 12, :, pl.ds(tile % 12 * LANES, LANES)]
    for j in range(NP // 2):
        tile = NP + j
        top = flow[tile // 12, :24, pl.ds(tile % 12 * LANES, LANES)]
        low = flow[tile // 12, 24:, pl.ds(tile % 12 * LANES, LANES)]
        psend[2 * j, ROWS:, :] = jnp.where(lane, top, pltpu.roll(low, 64, 1))
        psend[2 * j + 1, ROWS:, :] = jnp.where(lane, pltpu.roll(top, 64, 1), low)

    pl.semaphore_wait(barrier, NP - 1 + NG - 1)
    push("grp", me_g, NG, flow, grecv, 0, whole=False)
    push("pen", me_p, NP, psend, precv, 1)
    start = pl.multiple_of(lax.rem(me_g, 4) * 384, 128)
    grecv[me_g] = flow[lax.div(me_g, 4), :, pl.ds(start, 384)]
    precv[me_p] = psend[me_p]

    def fill(b, carry):
        rows = pl.ds(pl.multiple_of(b * 16, 16), 16)
        tah[rows, :] = pltpu.roll(rah[...], b * 16, 1).astype(BF16)
        tal[rows, :] = pltpu.roll(ral[...], b * 16, 1).astype(BF16)
        tbh[rows, :] = pltpu.roll(rbh[...], b * 16, 1)[:, :HALF].astype(BF16)
        tbl[rows, :] = pltpu.roll(rbl[...], b * 16, 1)[:, :HALF].astype(BF16)
        return carry
    lax.fori_loop(0, HALF // 16, fill, 0)

    for f in range(4):
        rows = pl.ds(f * ROWS, ROWS)
        one, two = flow[f, :, :HALF], flow[f, :, HALF:]
        xsh[rows, :], xsl[rows, :] = bf16_parts(one + two)
        xdh[rows, :], xdl[rows, :] = bf16_parts(one - two)

    def slopes(n, carry):
        cols = pl.ds(pl.multiple_of(n * 256, 256), 256)
        total = dot(xsh[...], tah[:, cols]) + dot(xsl[...], tah[:, cols]) + dot(xsh[...], tal[:, cols])
        other = dot(xdh[...], tbh[:, cols]) + dot(xdl[...], tbh[:, cols]) + dot(xdh[...], tbl[:, cols])
        for side, value in ((0, -(total + other)), (1, other - total)):
            where = pl.ds(pl.multiple_of(side * HALF + n * 256, 256), 256)
            along = flow[2, :, where]
            for i in range(3):
                slope = along * value[i * ROWS:(i + 1) * ROWS]
                if i == 2:
                    slope = slope + value[3 * ROWS:]
                pre[i, :, where] = flow[i, :, where] - 0.1 * slope
            div[:, where] = value[2 * ROWS:3 * ROWS]
        return carry
    lax.fori_loop(0, 3, slopes, 0)

    def places(s, carry):
        row = cells[pl.ds(s, 1), :] & (SPLIT - 1)
        def part(b, inner):
            index = lax.broadcasted_iota(jnp.int32, (16, MK), 0) + b * 16
            hot[s, pl.ds(pl.multiple_of(b * 16, 16), 16), :] = jnp.where(index == row, 1.0, 0.0).astype(BF16)
            return inner
        lax.fori_loop(0, SPLIT // 16, part, 0)
        return carry
    lax.fori_loop(0, ST, places, 0)

    upper, scale = elimination()
    arrived(grecv, NG, 0)

    def lines(t, carry):
        at = (pl.ds(pl.multiple_of(lax.div(t, 3) * 8, 8), 8), pl.ds(pl.multiple_of(lax.rem(t, 3) * LANES, LANES), LANES))
        f = [grecv[(i, *at)] for i in range(NG)]
        get = lambda i: f[i] if 0 <= i < NG else jnp.zeros_like(f[0])
        done = []
        for i in range(NG):
            value = (7.0 / 9.0) * (get(i + 1) - get(i - 1)) + (1.0 / 36.0) * (get(i + 2) - get(i - 2))
            if i:
                value = (value - done[-1] * (1.0 / 3.0)) * scale[i]
            done.append(value)
        value = done[-1]
        gmid[(NG - 1, *at)] = value
        for i in reversed(range(NG - 1)):
            value = done[i] - upper[i] * value
            gmid[(i, *at)] = value
        return carry
    lax.fori_loop(0, 18, lines, 0)
    push("grp", me_g, NG, gmid, gback, 2)
    gback[me_g] = gmid[me_g]

    arrived(precv, NP, 1)

    def halves(q, carry):
        rows = pl.ds(pl.multiple_of(q * ROWS, 16), ROWS)
        one, two = precv[q], precv[q + NP // 2]
        for high, low, value in ((fsh, fsl, one + two), (fdh, fdl, one - two)):
            packed = value[ROWS:]
            rest = jnp.concatenate([packed, pltpu.roll(packed, 64, 1)], axis=0)
            high[rows, :LANES], low[rows, :LANES] = bf16_parts(value[:ROWS])
            high[rows, LANES:], low[rows, LANES:] = bf16_parts(rest)
        return carry
    lax.fori_loop(0, NP // 2, halves, 0)

    def across(m, carry):
        rows = pl.ds(pl.multiple_of(m * 256, 256), 256)
        ysum[rows, :] = dot(tah[rows, :], fsh[...]) + dot(tah[rows, :], fsl[...]) + dot(tal[rows, :], fsh[...])
        ydif[rows, :] = dot(tbh[rows, :], fdh[...]) + dot(tbh[rows, :], fdl[...]) + dot(tbl[rows, :], fdh[...])
        return carry
    lax.fori_loop(0, 3, across, 0)

    def pieces(q, carry):
        rows = pl.ds(pl.multiple_of(q * ROWS, 8), ROWS)
        total, other = ysum[rows, :], ydif[rows, :]
        for slot, value in ((q, total + other), (q + NP // 2, total - other)):
            pmid[slot, :ROWS, :] = value[:, :LANES]
            rest = value[:, LANES:]
            pmid[slot, ROWS:, :] = jnp.where(lane, rest[:24], pltpu.roll(rest[24:], 64, 1))
        return carry
    lax.fori_loop(0, NP // 2, pieces, 0)
    push("pen", me_p, NP, pmid, pback, 3)
    pback[me_p] = pmid[me_p]

    arrived(gback, NG, 2)
    arrived(pback, NP, 3)
    for zt in range(12):
        cols = pl.ds(zt * LANES, LANES)
        d1 = []
        for f in range(4):
            tile = f * 12 + zt
            if tile < NP:
                d1.append(pback[tile, :ROWS, :])
            else:
                j = tile - NP
                one, two = pback[2 * j, ROWS:, :], pback[2 * j + 1, ROWS:, :]
                d1.append(jnp.concatenate([
                    jnp.where(lane, one, pltpu.roll(two, 64, 1)),
                    jnp.where(lane, pltpu.roll(one, 64, 1), two),
                ], axis=0))
        d0 = [gback[4 * f + zt // 3, :, pl.ds(zt % 3 * LANES, LANES)] for f in range(4)]
        u0, u1 = flow[0, :, cols], flow[1, :, cols]
        for i in range(3):
            slope = u0 * d0[i] + u1 * d1[i]
            if i == 0:
                slope = slope + d0[3]
            if i == 1:
                slope = slope + d1[3]
            value = pre[i, :, cols] - 0.1 * slope
            prov[i, :, cols] = value
            high, low = bf16_parts(value)
            rows = pl.ds((zt // 4 * 3 + i) * ROWS, ROWS)
            phi[rows, pl.ds(zt % 4 * LANES, LANES)] = high
            plo[rows, pl.ds(zt % 4 * LANES, LANES)] = low
        div[:, cols] = div[:, cols] + d0[0] + d1[1]

    wide = lax.broadcasted_iota(jnp.int32, (ROWS, LANES), 1)
    for g in range(NG):
        tile, off = divmod(96 * g, LANES)
        value = div[:, pl.ds(tile * LANES, LANES)]
        if off:
            value = pltpu.roll(value, LANES - off, 1)
        if off > 32:
            value = jnp.where(wide < LANES - off, value, pltpu.roll(div[:, pl.ds((tile + 1) * LANES, LANES)], LANES - off, 1))
        dsend[g] = value
    push("grp", me_g, NG, dsend, drecv, 4)
    drecv[me_g] = dsend[me_g]

    count = 3 * lax.broadcasted_iota(jnp.int32, (ROWS, MK), 0)
    acc[...] = jnp.zeros_like(acc)

    def sample(s, carry):
        place = hot[s]
        got = dot(phi[...], place) + dot(plo[...], place)
        code = cells[pl.ds(s, 1), :] >> 9
        weight = weights[pl.ds(s, 1), :]
        for i in range(3):
            total = None
            for zb in range(3):
                at = (zb * 3 + i) * ROWS
                picked = jnp.where(count + zb == code, got[at:at + ROWS], 0.0)
                picked = jnp.sum(picked.reshape(6, 8, MK), axis=0)
                total = picked if total is None else total + picked
            acc[i] += total * weight
        return carry
    lax.fori_loop(0, ST, sample, 0)
    sampled = [jnp.sum(acc[i], axis=0, keepdims=True) for i in range(3)]

    corr[...] = jnp.zeros_like(corr)

    def spread(s, carry):
        place = hot[s]
        code = cells[pl.ds(s, 1), :] >> 9
        weight = weights[pl.ds(s, 1), :]
        masks = [count + zb == code for zb in range(3)]
        parts = []
        for i in range(3):
            value = sampled[i] * weight
            high = value.astype(BF16).astype(F32)
            parts.append((high, (value - high).astype(BF16).astype(F32)))
        total = None
        for side in range(2):
            table = jnp.concatenate(
                [jnp.where(masks[zb], parts[i][side], 0.0).astype(BF16) for zb in range(3) for i in range(3)], axis=0
            )
            value = lax.dot_general(table, place, (((1,), (1,)), ((), ())), preferred_element_type=F32)
            total = value if total is None else total + value
        corr[...] += total
        return carry
    lax.fori_loop(0, ST, spread, 0)

    for zt in range(12):
        cols = pl.ds(zt * LANES, LANES)
        fluid = 1.0 - jnp.broadcast_to(solid[:, zt:zt + 1].astype(F32), (ROWS, LANES))
        for i in range(3):
            part = corr[pl.ds((zt // 4 * 3 + i) * ROWS, ROWS), pl.ds(zt % 4 * LANES, LANES)]
            vel[i, :, cols] = fluid * (prov[i, :, cols] - part)

    arrived(drecv, NG, 4)
    pois[...] = drecv[:, :, :96]

    sent(grecv, NG, 0)
    sent(psend, NP, 1)
    sent(gmid, NG, 2)
    sent(pmid, NP, 3)
    sent(dsend, NG, 4)


def body(flow_fields, marker_cells, marker_weights, solid_blocks):
    vmem = pl.BlockSpec(memory_space=pltpu.VMEM)
    tables = [jnp.asarray(rows) for rows in table_rows()]
    V = pltpu.VMEM
    velocity, source = pl.pallas_call(
        kernel,
        name="substep",
        out_shape=(
            jax.ShapeDtypeStruct((3, ROWS, NZ), F32),
            jax.ShapeDtypeStruct((NG, ROWS, 96), F32),
        ),
        in_specs=[vmem] * 8,
        out_specs=(vmem, vmem),
        scratch_shapes=[
            V((NP, PACK, LANES), F32), V((NP, PACK, LANES), F32), V((NP, PACK, LANES), F32), V((NP, PACK, LANES), F32),
            V((NG, ROWS, 384), F32), V((NG, ROWS, 384), F32), V((NG, ROWS, 384), F32),
            V((NG, ROWS, LANES), F32), V((NG, ROWS, LANES), F32),
            V((HALF, HALF), BF16), V((HALF, HALF), BF16), V((HALF, HALF), BF16), V((HALF, HALF), BF16),
            V((4 * ROWS, HALF), BF16), V((4 * ROWS, HALF), BF16), V((4 * ROWS, HALF), BF16), V((4 * ROWS, HALF), BF16),
            V((HALF, 256), F32), V((HALF, 256), F32),
            V((HALF, 256), BF16), V((HALF, 256), BF16), V((HALF, 256), BF16), V((HALF, 256), BF16),
            V((3, ROWS, NZ), F32), V((ROWS, NZ), F32), V((3, ROWS, NZ), F32),
            V((9 * ROWS, SPLIT), BF16), V((9 * ROWS, SPLIT), BF16),
            V((ST, SPLIT, MK), BF16), V((9 * ROWS, SPLIT), F32), V((3, 8, MK), F32),
            pltpu.SemaphoreType.DMA((5,)), pltpu.SemaphoreType.DMA((5,)),
        ],
        compiler_params=pltpu.CompilerParams(
            collective_id=0, has_side_effects=True, vmem_limit_bytes=60 * 1024 * 1024
        ),
    )(
        flow_fields.reshape(4, ROWS, NZ),
        marker_cells[0, 0].T,
        marker_weights[0, 0].T,
        solid_blocks[0],
        *tables,
    )
    return velocity.reshape(3, 1, ROWS, NZ), source


def solution(mesh):
    return jax.shard_map(
        body,
        mesh=mesh,
        in_specs=(
            P(None, "grp", "pen", None),
            P("grp", "pen", None, None),
            P("grp", "pen", None, None),
            P("grp", "pen", None),
        ),
        out_specs=(P(None, "grp", "pen", None), P(None, "pen", "grp")),
        check_vma=False,
    )
```

```python
import math

import jax
import jax.numpy as jnp
import numpy as np
from jax import lax
from jax.experimental import pallas as pl
from jax.experimental.pallas import tpu as pltpu
from jax.sharding import PartitionSpec as P

MESH = pl.DeviceIdType.MESH
F32, BF16 = jnp.float32, jnp.bfloat16
NG, NP = 16, 32
ROWS, NZ, HALF = 48, 1536, 768
LANES, SPLIT, MK, ST = 128, 512, 1024, 8
PARTS = NZ // SPLIT


def bf16_parts(values):
    high = values.astype(BF16)
    return high, (values - high.astype(F32)).astype(BF16)


def table_rows():
    lag = np.arange(2 * HALF)
    safe = np.where(lag % HALF == 0, 1, lag)
    line = math.pi / NZ * (1 - 2 * (lag % 2)) / np.tan(math.pi * safe / NZ)
    line = np.where(lag % HALF == 0, 0.0, line)
    other = np.roll(line, -HALF)
    rows = []
    for values, width in ((0.5 * (line + other), HALF), (0.5 * (line - other), 2 * HALF)):
        where = (np.arange(16)[:, None] - np.arange(width)[None, :]) % (2 * HALF)
        block = values[where].astype(np.float32)
        high = block.astype(jnp.bfloat16).astype(np.float32)
        rows += [high, (block - high).astype(jnp.bfloat16).astype(np.float32)]
    return rows


def elimination():
    upper, scale, last = [], [], 0.0
    for _ in range(NG):
        pivot = 1.0 / (1.0 - last / 3.0)
        last = pivot / 3.0
        upper.append(last)
        scale.append(pivot)
    return upper, scale


def kernel(
    flow, cells, weights, solid, rah, ral, rbh, rbl,
    vel, pois,
    psend, precv, pmid, pback, grecv, gmid, gback, dsend, drecv,
    tah, tal, tbh, tbl, xsh, xsl, xdh, xdl, ysum, ydif, fsum, fdif,
    pre, div, prov, phi, plo, hot, corr, acc, fluid,
    ssem, rsem,
):
    me_g, me_p = lax.axis_index("grp"), lax.axis_index("pen")
    lane = lax.broadcasted_iota(jnp.int32, (ROWS // 2, LANES), 1) < LANES // 2
    wide = lax.broadcasted_iota(jnp.int32, (ROWS, LANES), 1)
    dot = lambda a, b: jnp.dot(a, b, preferred_element_type=F32)
    swap = lambda value: pltpu.roll(value, LANES // 2, 1)
    barrier = pltpu.get_barrier_semaphore()

    def nth(k, middle, size):
        return lax.rem(middle + (1 - 2 * lax.rem(k, 2)) * lax.div(k + 1, 2), size)

    def pen_peer(t):
        z = lax.rem(lax.div(me_p, 2) + nth(lax.div(t, 4), 4, 8), 8)
        y = lax.rem(lax.div(me_p, 16) + 1 + lax.div(t, 2), 2)
        return y * 16 + z * 2 + lax.rem(me_p + t, 2)

    def grp_peer(t):
        x = lax.rem(me_g + nth(lax.div(t, 4), 2, 4), 4)
        y = lax.rem(lax.div(me_g, 4) + nth(lax.rem(t, 4), 2, 4), 4)
        return y * 4 + x

    def greet(axis, me, count):
        def step(d, carry):
            pl.semaphore_signal(
                barrier, 1, device_id={axis: lax.rem(me + d, count)}, device_id_type=MESH
            )
            return carry
        lax.fori_loop(1, count, step, 0)

    def push(axis, peer, src, dst, phase):
        pltpu.make_async_remote_copy(
            src_ref=src, dst_ref=dst, send_sem=ssem.at[phase], recv_sem=rsem.at[phase],
            device_id={axis: peer}, device_id_type=MESH,
        ).start()

    def exchange(to_pen, to_grp):
        def step(t, carry):
            to_pen(pen_peer(2 * t))
            to_pen(pen_peer(2 * t + 1))
            to_grp(grp_peer(t))
            return carry
        lax.fori_loop(0, NG - 1, step, 0)
        to_pen(pen_peer(NP - 1))

    def arrived(target, count, phase):
        ref = target.at[pl.ds(0, count - 1)]
        pltpu.make_async_copy(ref, ref, rsem.at[phase]).wait()

    def sent(source, count, phase):
        ref = source.at[pl.ds(0, count - 1)]
        pltpu.make_async_copy(ref, ref, ssem.at[phase]).wait()

    def mine(c, i):
        return flow.at[lax.div(i, 4), :, pl.ds(pl.multiple_of((lax.rem(i, 4) + 4 * c) * LANES, LANES), LANES)]

    greet("pen", me_p, NP)
    greet("grp", me_g, NG)

    for c in range(PARTS):
        for tile in range(16):
            cols = pl.ds((4 * c + tile % 4) * LANES, LANES)
            top, low = flow[tile // 4, :24, cols], flow[tile // 4, 24:, cols]
            psend[c, 2 * tile] = jnp.where(lane, top, swap(low))
            psend[c, 2 * tile + 1] = jnp.where(lane, swap(top), low)

    pl.semaphore_wait(barrier, NP - 1 + NG - 1)
    for c in range(PARTS):
        exchange(
            lambda peer: push("pen", peer, psend.at[c, peer], precv.at[c, me_p], c),
            lambda peer: push("grp", peer, mine(c, peer), grecv.at[c, me_g], PARTS + c),
        )
    for c in range(PARTS):
        precv[c, me_p] = psend[c, me_p]
        grecv[c, me_g] = mine(c, me_g)[...]

    def fill(b, carry):
        rows = pl.ds(pl.multiple_of(b * 16, 16), 16)
        tah[rows, :] = pltpu.roll(rah[...], b * 16, 1).astype(BF16)
        tal[rows, :] = pltpu.roll(ral[...], b * 16, 1).astype(BF16)
        tbh[rows, :] = pltpu.roll(rbh[...], b * 16, 1)[:, :HALF].astype(BF16)
        tbl[rows, :] = pltpu.roll(rbl[...], b * 16, 1)[:, :HALF].astype(BF16)
        return carry
    lax.fori_loop(0, HALF // 16, fill, 0)

    for f in range(4):
        rows = pl.ds(f * ROWS, ROWS)
        one, two = flow[f, :, :HALF], flow[f, :, HALF:]
        xsh[rows, :], xsl[rows, :] = bf16_parts(one + two)
        xdh[rows, :], xdl[rows, :] = bf16_parts(one - two)

    def slopes(n, carry):
        cols = pl.ds(pl.multiple_of(n * 256, 256), 256)
        total = dot(xsh[...], tah[:, cols]) + dot(xsl[...], tah[:, cols]) + dot(xsh[...], tal[:, cols])
        other = dot(xdh[...], tbh[:, cols]) + dot(xdl[...], tbh[:, cols]) + dot(xdh[...], tbl[:, cols])
        for side, value in ((0, -(total + other)), (1, other - total)):
            where = pl.ds(pl.multiple_of(side * HALF + n * 256, 256), 256)
            along = flow[2, :, where]
            for i in range(3):
                slope = along * value[i * ROWS:(i + 1) * ROWS]
                if i == 2:
                    slope = slope + value[3 * ROWS:]
                pre[i, :, where] = flow[i, :, where] - 0.1 * slope
            div[:, where] = value[2 * ROWS:3 * ROWS]
        return carry
    lax.fori_loop(0, 3, slopes, 0)

    def places(s, carry):
        row = cells[pl.ds(s, 1), :] & (SPLIT - 1)
        def part(b, inner):
            index = lax.broadcasted_iota(jnp.int32, (16, MK), 0) + b * 16
            hot[s, pl.ds(pl.multiple_of(b * 16, 16), 16), :] = jnp.where(index == row, 1.0, 0.0).astype(BF16)
            return inner
        lax.fori_loop(0, SPLIT // 16, part, 0)
        return carry
    lax.fori_loop(0, ST, places, 0)

    square = lax.broadcasted_iota(jnp.int32, (ROWS, ROWS), 0) == lax.broadcasted_iota(jnp.int32, (ROWS, ROWS), 1)
    for zt in range(12):
        open_cells = jnp.where(square, 1.0 - solid[zt].astype(F32), 0.0).astype(BF16)
        fluid[:, pl.ds(zt * LANES, LANES)] = dot(open_cells, jnp.ones((ROWS, LANES), BF16))

    upper, scale = elimination()
    for c in range(PARTS):
        arrived(grecv.at[c], NG, PARTS + c)

        def lines(t, carry):
            rows = pl.ds(pl.multiple_of(t * 8, 8), 8)
            f = [grecv[c, i, rows, :] for i in range(NG)]
            get = lambda i: f[i] if 0 <= i < NG else jnp.zeros_like(f[0])
            done = []
            for i in range(NG):
                value = (7.0 / 9.0) * (get(i + 1) - get(i - 1)) + (1.0 / 36.0) * (get(i + 2) - get(i - 2))
                if i:
                    value = (value - done[-1] * (1.0 / 3.0)) * scale[i]
                done.append(value)
            value = done[-1]
            gmid[c, NG - 1, rows, :] = value
            for i in reversed(range(NG - 1)):
                value = done[i] - upper[i] * value
                gmid[c, i, rows, :] = value
            return carry
        lax.fori_loop(0, ROWS // 8, lines, 0)
        gback[c, me_g] = gmid[c, me_g]

        arrived(precv.at[c], NP, c)

        def halves(q, carry):
            rows = pl.ds(pl.multiple_of(q * ROWS, 16), ROWS)
            one, two = precv[c, q], precv[c, q + NP // 2]
            for both, packed in ((fsum, one + two), (fdif, one - two)):
                value = jnp.concatenate([packed, swap(packed)], axis=0)
                high = value.astype(BF16).astype(F32)
                both[rows, :] = jnp.where(wide < LANES // 2, high, swap(value - high)).astype(BF16)
            return carry
        lax.fori_loop(0, NP // 2, halves, 0)

        def across(m, carry):
            rows = pl.ds(pl.multiple_of(m * 256, 256), 256)
            for out, high, low, both in ((ysum, tah, tal, fsum), (ydif, tbh, tbl, fdif)):
                value = dot(high[rows, :], both[...])
                out[rows, :] = value + swap(value) + dot(low[rows, :], both[...])
            return carry
        lax.fori_loop(0, 3, across, 0)

        def pieces(q, carry):
            rows = pl.ds(pl.multiple_of(q * ROWS, 8), ROWS)
            total, other = ysum[rows, :], ydif[rows, :]
            for slot, value in ((q, total + other), (q + NP // 2, total - other)):
                pmid[c, slot] = jnp.where(lane, value[:24], swap(value[24:]))
            return carry
        lax.fori_loop(0, NP // 2, pieces, 0)
        exchange(
            lambda peer: push("pen", peer, pmid.at[c, peer], pback.at[c, me_p], 2 * PARTS + c),
            lambda peer: push("grp", peer, gmid.at[c, peer], gback.at[c, me_g], 3 * PARTS + c),
        )
        pback[c, me_p] = pmid[c, me_p]

    count = 3 * lax.broadcasted_iota(jnp.int32, (ROWS, MK), 0)
    acc[...] = jnp.zeros_like(acc)
    corr[...] = jnp.zeros_like(corr)
    for c in range(PARTS):
        arrived(gback.at[c], NG, 3 * PARTS + c)
        arrived(pback.at[c], NP, 2 * PARTS + c)
        for k in range(4):
            cols = pl.ds((4 * c + k) * LANES, LANES)
            d0 = [gback[c, 4 * f + k] for f in range(4)]
            d1 = []
            for f in range(4):
                one, two = pback[c, 8 * f + 2 * k], pback[c, 8 * f + 2 * k + 1]
                d1.append(jnp.concatenate([jnp.where(lane, one, swap(two)), jnp.where(lane, swap(one), two)], axis=0))
            u0, u1 = flow[0, :, cols], flow[1, :, cols]
            for i in range(3):
                slope = u0 * d0[i] + u1 * d1[i]
                if i == 0:
                    slope = slope + d0[3]
                if i == 1:
                    slope = slope + d1[3]
                value = pre[i, :, cols] - 0.1 * slope
                prov[i, :, cols] = value
                rows = pl.ds((3 * c + i) * ROWS, ROWS)
                phi[rows, pl.ds(k * LANES, LANES)], plo[rows, pl.ds(k * LANES, LANES)] = bf16_parts(value)
            div[:, cols] = div[:, cols] + d0[0] + d1[1]

        if c == PARTS - 1:
            for g in range(NG):
                tile, off = divmod(96 * g, LANES)
                value = div[:, pl.ds(tile * LANES, LANES)]
                if off:
                    value = pltpu.roll(value, LANES - off, 1)
                if off > 32:
                    rest = pltpu.roll(div[:, pl.ds((tile + 1) * LANES, LANES)], LANES - off, 1)
                    value = jnp.where(wide < LANES - off, value, rest)
                dsend[g] = value

            def spread_out(t, carry):
                peer = grp_peer(t)
                push("grp", peer, dsend.at[peer], drecv.at[me_g], 4 * PARTS)
                return carry
            lax.fori_loop(0, NG - 1, spread_out, 0)
            drecv[me_g] = dsend[me_g]

        def sample(s, carry):
            place = hot[s]
            rows = pl.ds(3 * c * ROWS, 3 * ROWS)
            got = dot(phi[rows, :], place) + dot(plo[rows, :], place)
            mask = count + c == cells[pl.ds(s, 1), :] >> 9
            weight = weights[pl.ds(s, 1), :]
            for i in range(3):
                picked = jnp.where(mask, got[i * ROWS:(i + 1) * ROWS], 0.0)
                acc[i] += jnp.sum(picked.reshape(6, 8, MK), axis=0) * weight
            return carry
        lax.fori_loop(0, ST, sample, 0)

    sampled = [jnp.sum(acc[i], axis=0, keepdims=True) for i in range(3)]

    def spread(s, carry):
        place = hot[s]
        code = cells[pl.ds(s, 1), :] >> 9
        weight = weights[pl.ds(s, 1), :]
        masks = [count + zb == code for zb in range(3)]
        parts = []
        for i in range(3):
            value = sampled[i] * weight
            high = value.astype(BF16).astype(F32)
            parts.append((high, (value - high).astype(BF16).astype(F32)))
        total = None
        for side in range(2):
            table = jnp.concatenate(
                [jnp.where(masks[zb], parts[i][side], 0.0).astype(BF16) for zb in range(3) for i in range(3)], axis=0
            )
            value = lax.dot_general(table, place, (((1,), (1,)), ((), ())), preferred_element_type=F32)
            total = value if total is None else total + value
        corr[...] += total
        return carry
    lax.fori_loop(0, ST, spread, 0)

    for zt in range(12):
        cols = pl.ds(zt * LANES, LANES)
        for i in range(3):
            part = corr[pl.ds((zt // 4 * 3 + i) * ROWS, ROWS), pl.ds(zt % 4 * LANES, LANES)]
            vel[i, :, cols] = fluid[:, cols] * (prov[i, :, cols] - part)

    arrived(drecv, NG, 4 * PARTS)
    pois[...] = drecv[:, :, :96]

    for c in range(PARTS):
        sent(psend.at[c], NP, c)
        sent(grecv.at[c], NG, PARTS + c)
        sent(pmid.at[c], NP, 2 * PARTS + c)
        sent(gmid.at[c], NG, 3 * PARTS + c)
    sent(dsend, NG, 4 * PARTS)


def body(flow_fields, marker_cells, marker_weights, solid_blocks):
    vmem = pl.BlockSpec(memory_space=pltpu.VMEM)
    tables = [jnp.asarray(rows) for rows in table_rows()]
    V = pltpu.VMEM
    velocity, source = pl.pallas_call(
        kernel,
        name="substep",
        out_shape=(
            jax.ShapeDtypeStruct((3, ROWS, NZ), F32),
            jax.ShapeDtypeStruct((NG, ROWS, 96), F32),
        ),
        in_specs=[vmem] * 8,
        out_specs=(vmem, vmem),
        scratch_shapes=[
            *[V((PARTS, NP, ROWS // 2, LANES), F32)] * 4,
            *[V((PARTS, NG, ROWS, LANES), F32)] * 3,
            V((NG, ROWS, LANES), F32), V((NG, ROWS, LANES), F32),
            V((HALF, HALF), BF16), V((HALF, HALF), BF16), V((HALF, HALF), BF16), V((HALF, HALF), BF16),
            V((4 * ROWS, HALF), BF16), V((4 * ROWS, HALF), BF16), V((4 * ROWS, HALF), BF16), V((4 * ROWS, HALF), BF16),
            V((HALF, LANES), F32), V((HALF, LANES), F32), V((HALF, LANES), BF16), V((HALF, LANES), BF16),
            V((3, ROWS, NZ), F32), V((ROWS, NZ), F32), V((3, ROWS, NZ), F32),
            V((9 * ROWS, SPLIT), BF16), V((9 * ROWS, SPLIT), BF16),
            V((ST, SPLIT, MK), BF16), V((9 * ROWS, SPLIT), F32), V((3, 8, MK), F32), V((ROWS, NZ), F32),
            pltpu.SemaphoreType.DMA((4 * PARTS + 1,)), pltpu.SemaphoreType.DMA((4 * PARTS + 1,)),
        ],
        compiler_params=pltpu.CompilerParams(
            collective_id=0, has_side_effects=True, vmem_limit_bytes=60 * 1024 * 1024
        ),
    )(
        flow_fields.reshape(4, ROWS, NZ),
        marker_cells[0, 0].T,
        marker_weights[0, 0].T,
        solid_blocks.transpose(2, 0, 1),
        *tables,
    )
    return velocity.reshape(3, 1, ROWS, NZ), source


def solution(mesh):
    return jax.shard_map(
        body,
        mesh=mesh,
        in_specs=(
            P(None, "grp", "pen", None),
            P("grp", "pen", None, None),
            P("grp", "pen", None, None),
            P("grp", "pen", None),
        ),
        out_specs=(P(None, "grp", "pen", None), P(None, "pen", "grp")),
        check_vma=False,
    )
```

```python
import math

import jax
import jax.numpy as jnp
import numpy as np
from jax import lax
from jax.experimental import pallas as pl
from jax.experimental.pallas import tpu as pltpu
from jax.sharding import PartitionSpec as P

MESH = pl.DeviceIdType.MESH
F32, BF16 = jnp.float32, jnp.bfloat16
NG, NP = 16, 32
ROWS, NZ, HALF = 48, 1536, 768
LANES, SPLIT, MK, ST = 128, 512, 1024, 8
PARTS = NZ // SPLIT


def bf16_parts(values):
    high = values.astype(BF16)
    return high, (values - high.astype(F32)).astype(BF16)


def table_rows():
    lag = np.arange(2 * HALF)
    safe = np.where(lag % HALF == 0, 1, lag)
    line = math.pi / NZ * (1 - 2 * (lag % 2)) / np.tan(math.pi * safe / NZ)
    line = np.where(lag % HALF == 0, 0.0, line)
    other = np.roll(line, -HALF)
    rows = []
    for values, width in ((0.5 * (line + other), HALF), (0.5 * (line - other), 2 * HALF)):
        where = (np.arange(16)[:, None] - np.arange(width)[None, :]) % (2 * HALF)
        block = values[where].astype(np.float32)
        high = block.astype(jnp.bfloat16).astype(np.float32)
        rows += [high, (block - high).astype(jnp.bfloat16).astype(np.float32)]
    return rows


def elimination():
    upper, scale, last = [], [], 0.0
    for _ in range(NG):
        pivot = 1.0 / (1.0 - last / 3.0)
        last = pivot / 3.0
        upper.append(last)
        scale.append(pivot)
    return upper, scale


def kernel(
    source, cells, weights, solid, rah, ral, rbh, rbl,
    vel, pois,
    flow, psend, precv, pmid, pback, grecv, gmid, gback, dsend, drecv,
    tah, tal, tbh, tbl, xsh, xsl, xdh, xdl, ysum, ydif, fsum, fdif,
    pre, div, prov, phi, plo, hot, corr, acc, fluid,
    ssem, rsem, fsem,
):
    me_g, me_p = lax.axis_index("grp"), lax.axis_index("pen")
    lane = lax.broadcasted_iota(jnp.int32, (ROWS // 2, LANES), 1) < LANES // 2
    wide = lax.broadcasted_iota(jnp.int32, (ROWS, LANES), 1)
    dot = lambda a, b: jnp.dot(a, b, preferred_element_type=F32)
    swap = lambda value: pltpu.roll(value, LANES // 2, 1)
    barrier = pltpu.get_barrier_semaphore()

    def nth(k, middle, size):
        return lax.rem(middle + (1 - 2 * lax.rem(k, 2)) * lax.div(k + 1, 2), size)

    def pen_peer(t):
        z = lax.rem(lax.div(me_p, 2) + nth(lax.div(t, 4), 4, 8), 8)
        y = lax.rem(lax.div(me_p, 16) + 1 + lax.div(t, 2), 2)
        return y * 16 + z * 2 + lax.rem(me_p + t, 2)

    def grp_peer(t):
        x = lax.rem(me_g + nth(lax.div(t, 4), 2, 4), 4)
        y = lax.rem(lax.div(me_g, 4) + nth(lax.rem(t, 4), 2, 4), 4)
        return y * 4 + x

    def greet(axis, me, count):
        def step(d, carry):
            pl.semaphore_signal(
                barrier, 1, device_id={axis: lax.rem(me + d, count)}, device_id_type=MESH
            )
            return carry
        lax.fori_loop(1, count, step, 0)

    def push(axis, peer, src, dst, phase):
        pltpu.make_async_remote_copy(
            src_ref=src, dst_ref=dst, send_sem=ssem.at[phase], recv_sem=rsem.at[phase],
            device_id={axis: peer}, device_id_type=MESH,
        ).start()

    def exchange(to_pen, to_grp):
        def step(t, carry):
            to_pen(pen_peer(2 * t))
            to_pen(pen_peer(2 * t + 1))
            to_grp(grp_peer(t))
            return carry
        lax.fori_loop(0, NG - 1, step, 0)
        to_pen(pen_peer(NP - 1))

    def arrived(target, count, phase):
        ref = target.at[pl.ds(0, count - 1)]
        pltpu.make_async_copy(ref, ref, rsem.at[phase]).wait()

    def sent(source, count, phase):
        ref = source.at[pl.ds(0, count - 1)]
        pltpu.make_async_copy(ref, ref, ssem.at[phase]).wait()

    def mine(c, i):
        return flow.at[lax.div(i, 4), :, pl.ds(pl.multiple_of((lax.rem(i, 4) + 4 * c) * LANES, LANES), LANES)]

    fetch = pltpu.make_async_copy(source, flow, fsem)
    fetch.start()
    greet("pen", me_p, NP)
    greet("grp", me_g, NG)
    fetch.wait()

    for c in range(PARTS):
        for tile in range(16):
            cols = pl.ds((4 * c + tile % 4) * LANES, LANES)
            top, low = flow[tile // 4, :24, cols], flow[tile // 4, 24:, cols]
            psend[c, 2 * tile] = jnp.where(lane, top, swap(low))
            psend[c, 2 * tile + 1] = jnp.where(lane, swap(top), low)

    pl.semaphore_wait(barrier, NP - 1 + NG - 1)
    for c in range(PARTS):
        exchange(
            lambda peer: push("pen", peer, psend.at[c, peer], precv.at[c, me_p], c),
            lambda peer: push("grp", peer, mine(c, peer), grecv.at[c, me_g], PARTS + c),
        )
    for c in range(PARTS):
        precv[c, me_p] = psend[c, me_p]
        grecv[c, me_g] = mine(c, me_g)[...]

    def fill(b, carry):
        rows = pl.ds(pl.multiple_of(b * 16, 16), 16)
        tah[rows, :] = pltpu.roll(rah[...], b * 16, 1).astype(BF16)
        tal[rows, :] = pltpu.roll(ral[...], b * 16, 1).astype(BF16)
        tbh[rows, :] = pltpu.roll(rbh[...], b * 16, 1)[:, :HALF].astype(BF16)
        tbl[rows, :] = pltpu.roll(rbl[...], b * 16, 1)[:, :HALF].astype(BF16)
        return carry
    lax.fori_loop(0, HALF // 16, fill, 0)

    for f in range(4):
        rows = pl.ds(f * ROWS, ROWS)
        one, two = flow[f, :, :HALF], flow[f, :, HALF:]
        xsh[rows, :], xsl[rows, :] = bf16_parts(one + two)
        xdh[rows, :], xdl[rows, :] = bf16_parts(one - two)

    def slopes(n, carry):
        cols = pl.ds(pl.multiple_of(n * 256, 256), 256)
        total = dot(xsh[...], tah[:, cols]) + dot(xsl[...], tah[:, cols]) + dot(xsh[...], tal[:, cols])
        other = dot(xdh[...], tbh[:, cols]) + dot(xdl[...], tbh[:, cols]) + dot(xdh[...], tbl[:, cols])
        for side, value in ((0, -(total + other)), (1, other - total)):
            where = pl.ds(pl.multiple_of(side * HALF + n * 256, 256), 256)
            along = flow[2, :, where]
            for i in range(3):
                slope = along * value[i * ROWS:(i + 1) * ROWS]
                if i == 2:
                    slope = slope + value[3 * ROWS:]
                pre[i, :, where] = flow[i, :, where] - 0.1 * slope
            div[:, where] = value[2 * ROWS:3 * ROWS]
        return carry
    lax.fori_loop(0, 3, slopes, 0)

    def places(s, carry):
        row = cells[pl.ds(s, 1), :] & (SPLIT - 1)
        def part(b, inner):
            index = lax.broadcasted_iota(jnp.int32, (16, MK), 0) + b * 16
            hot[s, pl.ds(pl.multiple_of(b * 16, 16), 16), :] = jnp.where(index == row, 1.0, 0.0).astype(BF16)
            return inner
        lax.fori_loop(0, SPLIT // 16, part, 0)
        return carry
    lax.fori_loop(0, ST, places, 0)

    square = lax.broadcasted_iota(jnp.int32, (ROWS, ROWS), 0) == lax.broadcasted_iota(jnp.int32, (ROWS, ROWS), 1)
    for zt in range(12):
        open_cells = jnp.where(square, 1.0 - solid[zt].astype(F32), 0.0).astype(BF16)
        fluid[:, pl.ds(zt * LANES, LANES)] = dot(open_cells, jnp.ones((ROWS, LANES), BF16))

    upper, scale = elimination()
    for c in range(PARTS):
        arrived(grecv.at[c], NG, PARTS + c)

        def lines(t, carry):
            rows = pl.ds(pl.multiple_of(t * 8, 8), 8)
            f = [grecv[c, i, rows, :] for i in range(NG)]
            get = lambda i: f[i] if 0 <= i < NG else jnp.zeros_like(f[0])
            done = []
            for i in range(NG):
                value = (7.0 / 9.0) * (get(i + 1) - get(i - 1)) + (1.0 / 36.0) * (get(i + 2) - get(i - 2))
                if i:
                    value = (value - done[-1] * (1.0 / 3.0)) * scale[i]
                done.append(value)
            value = done[-1]
            gmid[c, NG - 1, rows, :] = value
            for i in reversed(range(NG - 1)):
                value = done[i] - upper[i] * value
                gmid[c, i, rows, :] = value
            return carry
        lax.fori_loop(0, ROWS // 8, lines, 0)
        gback[c, me_g] = gmid[c, me_g]

        arrived(precv.at[c], NP, c)

        def halves(q, carry):
            rows = pl.ds(pl.multiple_of(q * ROWS, 16), ROWS)
            one, two = precv[c, q], precv[c, q + NP // 2]
            for both, packed in ((fsum, one + two), (fdif, one - two)):
                value = jnp.concatenate([packed, swap(packed)], axis=0)
                high = value.astype(BF16).astype(F32)
                both[rows, :] = jnp.where(wide < LANES // 2, high, swap(value - high)).astype(BF16)
            return carry
        lax.fori_loop(0, NP // 2, halves, 0)

        def across(m, carry):
            rows = pl.ds(pl.multiple_of(m * 256, 256), 256)
            for out, high, low, both in ((ysum, tah, tal, fsum), (ydif, tbh, tbl, fdif)):
                value = dot(high[rows, :], both[...])
                out[rows, :] = value + swap(value) + dot(low[rows, :], both[...])
            return carry
        lax.fori_loop(0, 3, across, 0)

        def pieces(q, carry):
            rows = pl.ds(pl.multiple_of(q * ROWS, 8), ROWS)
            total, other = ysum[rows, :], ydif[rows, :]
            for slot, value in ((q, total + other), (q + NP // 2, total - other)):
                pmid[c, slot] = jnp.where(lane, value[:24], swap(value[24:]))
            return carry
        lax.fori_loop(0, NP // 2, pieces, 0)
        exchange(
            lambda peer: push("pen", peer, pmid.at[c, peer], pback.at[c, me_p], 2 * PARTS + c),
            lambda peer: push("grp", peer, gmid.at[c, peer], gback.at[c, me_g], 3 * PARTS + c),
        )
        pback[c, me_p] = pmid[c, me_p]

    count = 3 * lax.broadcasted_iota(jnp.int32, (ROWS, MK), 0)
    acc[...] = jnp.zeros_like(acc)
    corr[...] = jnp.zeros_like(corr)
    for c in range(PARTS):
        arrived(gback.at[c], NG, 3 * PARTS + c)
        arrived(pback.at[c], NP, 2 * PARTS + c)
        for k in range(4):
            cols = pl.ds((4 * c + k) * LANES, LANES)
            d0 = [gback[c, 4 * f + k] for f in range(4)]
            d1 = []
            for f in range(4):
                one, two = pback[c, 8 * f + 2 * k], pback[c, 8 * f + 2 * k + 1]
                d1.append(jnp.concatenate([jnp.where(lane, one, swap(two)), jnp.where(lane, swap(one), two)], axis=0))
            u0, u1 = flow[0, :, cols], flow[1, :, cols]
            for i in range(3):
                slope = u0 * d0[i] + u1 * d1[i]
                if i == 0:
                    slope = slope + d0[3]
                if i == 1:
                    slope = slope + d1[3]
                value = pre[i, :, cols] - 0.1 * slope
                prov[i, :, cols] = value
                rows = pl.ds((3 * c + i) * ROWS, ROWS)
                phi[rows, pl.ds(k * LANES, LANES)], plo[rows, pl.ds(k * LANES, LANES)] = bf16_parts(value)
            div[:, cols] = div[:, cols] + d0[0] + d1[1]

        if c == PARTS - 1:
            for g in range(NG):
                tile, off = divmod(96 * g, LANES)
                value = div[:, pl.ds(tile * LANES, LANES)]
                if off:
                    value = pltpu.roll(value, LANES - off, 1)
                if off > 32:
                    rest = pltpu.roll(div[:, pl.ds((tile + 1) * LANES, LANES)], LANES - off, 1)
                    value = jnp.where(wide < LANES - off, value, rest)
                dsend[g] = value

            def spread_out(t, carry):
                peer = grp_peer(t)
                push("grp", peer, dsend.at[peer], drecv.at[me_g], 4 * PARTS)
                return carry
            lax.fori_loop(0, NG - 1, spread_out, 0)
            drecv[me_g] = dsend[me_g]

        def sample(s, carry):
            place = hot[s]
            rows = pl.ds(3 * c * ROWS, 3 * ROWS)
            got = dot(phi[rows, :], place) + dot(plo[rows, :], place)
            mask = count + c == cells[pl.ds(s, 1), :] >> 9
            weight = weights[pl.ds(s, 1), :]
            for i in range(3):
                picked = jnp.where(mask, got[i * ROWS:(i + 1) * ROWS], 0.0)
                acc[i] += jnp.sum(picked.reshape(6, 8, MK), axis=0) * weight
            return carry
        lax.fori_loop(0, ST, sample, 0)

    sampled = [jnp.sum(acc[i], axis=0, keepdims=True) for i in range(3)]

    def spread(s, carry):
        place = hot[s]
        code = cells[pl.ds(s, 1), :] >> 9
        weight = weights[pl.ds(s, 1), :]
        masks = [count + zb == code for zb in range(3)]
        parts = []
        for i in range(3):
            value = sampled[i] * weight
            high = value.astype(BF16).astype(F32)
            parts.append((high, (value - high).astype(BF16).astype(F32)))
        total = None
        for side in range(2):
            table = jnp.concatenate(
                [jnp.where(masks[zb], parts[i][side], 0.0).astype(BF16) for zb in range(3) for i in range(3)], axis=0
            )
            value = lax.dot_general(table, place, (((1,), (1,)), ((), ())), preferred_element_type=F32)
            total = value if total is None else total + value
        corr[...] += total
        return carry
    lax.fori_loop(0, ST, spread, 0)

    for zt in range(12):
        cols = pl.ds(zt * LANES, LANES)
        for i in range(3):
            part = corr[pl.ds((zt // 4 * 3 + i) * ROWS, ROWS), pl.ds(zt % 4 * LANES, LANES)]
            vel[i, :, cols] = fluid[:, cols] * (prov[i, :, cols] - part)

    arrived(drecv, NG, 4 * PARTS)
    pois[...] = drecv[:, :, :96]

    for c in range(PARTS):
        sent(psend.at[c], NP, c)
        sent(grecv.at[c], NG, PARTS + c)
        sent(pmid.at[c], NP, 2 * PARTS + c)
        sent(gmid.at[c], NG, 3 * PARTS + c)
    sent(dsend, NG, 4 * PARTS)


def body(flow_fields, marker_cells, marker_weights, solid_blocks):
    vmem = pl.BlockSpec(memory_space=pltpu.VMEM)
    tables = [jnp.asarray(rows) for rows in table_rows()]
    V = pltpu.VMEM
    velocity, source = pl.pallas_call(
        kernel,
        name="substep",
        out_shape=(
            pltpu.VMEM((3, ROWS, NZ), F32),
            pltpu.VMEM((NG, ROWS, 96), F32),
        ),
        in_specs=[pl.BlockSpec(memory_space=pl.ANY)] + [vmem] * 7,
        out_specs=(vmem, vmem),
        scratch_shapes=[
            V((4, ROWS, NZ), F32),
            *[V((PARTS, NP, ROWS // 2, LANES), F32)] * 4,
            *[V((PARTS, NG, ROWS, LANES), F32)] * 3,
            V((NG, ROWS, LANES), F32), V((NG, ROWS, LANES), F32),
            V((HALF, HALF), BF16), V((HALF, HALF), BF16), V((HALF, HALF), BF16), V((HALF, HALF), BF16),
            V((4 * ROWS, HALF), BF16), V((4 * ROWS, HALF), BF16), V((4 * ROWS, HALF), BF16), V((4 * ROWS, HALF), BF16),
            V((HALF, LANES), F32), V((HALF, LANES), F32), V((HALF, LANES), BF16), V((HALF, LANES), BF16),
            V((3, ROWS, NZ), F32), V((ROWS, NZ), F32), V((3, ROWS, NZ), F32),
            V((9 * ROWS, SPLIT), BF16), V((9 * ROWS, SPLIT), BF16),
            V((ST, SPLIT, MK), BF16), V((9 * ROWS, SPLIT), F32), V((3, 8, MK), F32), V((ROWS, NZ), F32),
            pltpu.SemaphoreType.DMA((4 * PARTS + 1,)), pltpu.SemaphoreType.DMA((4 * PARTS + 1,)),
            pltpu.SemaphoreType.DMA,
        ],
        compiler_params=pltpu.CompilerParams(
            collective_id=0, has_side_effects=True, vmem_limit_bytes=60 * 1024 * 1024
        ),
    )(
        flow_fields.reshape(4, ROWS, NZ),
        marker_cells[0, 0].T,
        marker_weights[0, 0].T,
        solid_blocks.transpose(2, 0, 1),
        *tables,
    )
    return velocity.reshape(3, 1, ROWS, NZ), source


def solution(mesh):
    return jax.shard_map(
        body,
        mesh=mesh,
        in_specs=(
            P(None, "grp", "pen", None),
            P("grp", "pen", None, None),
            P("grp", "pen", None, None),
            P("grp", "pen", None),
        ),
        out_specs=(P(None, "grp", "pen", None), P(None, "pen", "grp")),
        check_vma=False,
    )
```

```python
import math

import jax
import jax.numpy as jnp
import numpy as np
from jax import lax
from jax.experimental import pallas as pl
from jax.experimental.pallas import tpu as pltpu
from jax.sharding import PartitionSpec as P

MESH = pl.DeviceIdType.MESH
F32, BF16 = jnp.float32, jnp.bfloat16
NG, NP = 16, 32
ROWS, NZ, HALF = 48, 1536, 768
LANES, SPLIT, MK, ST = 128, 512, 1024, 8
PARTS = NZ // SPLIT
GROUPS = ((0, 2), (2, 1))


def bf16_parts(values):
    high = values.astype(BF16)
    return high, (values - high.astype(F32)).astype(BF16)


def table_rows():
    lag = np.arange(2 * HALF)
    safe = np.where(lag % HALF == 0, 1, lag)
    line = math.pi / NZ * (1 - 2 * (lag % 2)) / np.tan(math.pi * safe / NZ)
    line = np.where(lag % HALF == 0, 0.0, line)
    other = np.roll(line, -HALF)
    rows = []
    for values, width in ((0.5 * (line + other), HALF), (0.5 * (line - other), 2 * HALF)):
        where = (np.arange(16)[:, None] - np.arange(width)[None, :]) % (2 * HALF)
        block = values[where].astype(np.float32)
        high = block.astype(jnp.bfloat16).astype(np.float32)
        rows += [high, (block - high).astype(jnp.bfloat16).astype(np.float32)]
    return rows


def elimination():
    upper, scale, last = [], [], 0.0
    for _ in range(NG):
        pivot = 1.0 / (1.0 - last / 3.0)
        last = pivot / 3.0
        upper.append(last)
        scale.append(pivot)
    return upper, scale


def kernel(
    source, cells, weights, solid, rah, ral, rbh, rbl,
    vel, pois,
    flow, psend, precv, pmid, pback, grecv, gmid, gback, dsend, drecv,
    tah, tal, tbh, tbl, xsh, xsl, xdh, xdl, ysum, ydif, fsum, fdif,
    pre, div, prov, phi, plo, hot, corr, acc, fluid,
    ssem, rsem, fsem,
):
    me_g, me_p = lax.axis_index("grp"), lax.axis_index("pen")
    lane = lax.broadcasted_iota(jnp.int32, (ROWS // 2, LANES), 1) < LANES // 2
    wide = lax.broadcasted_iota(jnp.int32, (ROWS, LANES), 1)
    dot = lambda a, b: jnp.dot(a, b, preferred_element_type=F32)
    swap = lambda value: pltpu.roll(value, LANES // 2, 1)
    barrier = pltpu.get_barrier_semaphore()

    def nth(k, middle, size):
        return lax.rem(middle + (1 - 2 * lax.rem(k, 2)) * lax.div(k + 1, 2), size)

    def pen_peer(t):
        z = lax.rem(lax.div(me_p, 2) + nth(lax.div(t, 4), 4, 8), 8)
        y = lax.rem(lax.div(me_p, 16) + 1 + lax.div(t, 2), 2)
        return y * 16 + z * 2 + lax.rem(me_p + t, 2)

    def grp_peer(t):
        x = lax.rem(me_g + nth(lax.div(t, 4), 2, 4), 4)
        y = lax.rem(lax.div(me_g, 4) + nth(lax.rem(t, 4), 2, 4), 4)
        return y * 4 + x

    def greet(axis, me, count):
        def step(d, carry):
            pl.semaphore_signal(
                barrier, 1, device_id={axis: lax.rem(me + d, count)}, device_id_type=MESH
            )
            return carry
        lax.fori_loop(1, count, step, 0)

    def push(axis, peer, src, dst, phase):
        pltpu.make_async_remote_copy(
            src_ref=src, dst_ref=dst, send_sem=ssem.at[phase], recv_sem=rsem.at[phase],
            device_id={axis: peer}, device_id_type=MESH,
        ).start()

    def exchange(to_pen, to_grp):
        def step(t, carry):
            to_pen(pen_peer(2 * t))
            to_pen(pen_peer(2 * t + 1))
            to_grp(grp_peer(t))
            return carry
        lax.fori_loop(0, NG - 1, step, 0)
        to_pen(pen_peer(NP - 1))

    def pen_block(ref, slot, group):
        return ref.at[slot, pl.ds(*GROUPS[group])]

    def grp_block(ref, slot, group):
        first, size = GROUPS[group]
        return ref.at[slot, :, pl.ds(first * LANES, size * LANES)]

    def arrived(ref, phase):
        pltpu.make_async_copy(ref, ref, rsem.at[phase]).wait()

    def sent(ref, phase):
        pltpu.make_async_copy(ref, ref, ssem.at[phase]).wait()

    def mine(i, group):
        first, size = GROUPS[group]
        start = pl.multiple_of((4 * first + size * lax.rem(i, 4)) * LANES, LANES)
        return flow.at[lax.div(i, 4), :, pl.ds(start, size * LANES)]

    fetch = pltpu.make_async_copy(source, flow, fsem)
    fetch.start()
    greet("pen", me_p, NP)
    greet("grp", me_g, NG)
    fetch.wait()

    for c in range(PARTS):
        for tile in range(16):
            cols = pl.ds((4 * c + tile % 4) * LANES, LANES)
            top, low = flow[tile // 4, :24, cols], flow[tile // 4, 24:, cols]
            psend[2 * tile, c] = jnp.where(lane, top, swap(low))
            psend[2 * tile + 1, c] = jnp.where(lane, swap(top), low)

    pl.semaphore_wait(barrier, NP - 1 + NG - 1)
    for group, (first, size) in enumerate(GROUPS):
        exchange(
            lambda peer: push("pen", peer, pen_block(psend, peer, group), pen_block(precv, me_p, group), group),
            lambda peer: push("grp", peer, mine(peer, group), grp_block(grecv, me_g, group), 2 + group),
        )
    precv[me_p] = psend[me_p]
    for group, (first, size) in enumerate(GROUPS):
        grecv[me_g, :, pl.ds(first * LANES, size * LANES)] = mine(me_g, group)[...]

    def fill(b, carry):
        rows = pl.ds(pl.multiple_of(b * 16, 16), 16)
        tah[rows, :] = pltpu.roll(rah[...], b * 16, 1).astype(BF16)
        tal[rows, :] = pltpu.roll(ral[...], b * 16, 1).astype(BF16)
        tbh[rows, :] = pltpu.roll(rbh[...], b * 16, 1)[:, :HALF].astype(BF16)
        tbl[rows, :] = pltpu.roll(rbl[...], b * 16, 1)[:, :HALF].astype(BF16)
        return carry
    lax.fori_loop(0, HALF // 16, fill, 0)

    for f in range(4):
        rows = pl.ds(f * ROWS, ROWS)
        one, two = flow[f, :, :HALF], flow[f, :, HALF:]
        xsh[rows, :], xsl[rows, :] = bf16_parts(one + two)
        xdh[rows, :], xdl[rows, :] = bf16_parts(one - two)

    def slopes(n, carry):
        cols = pl.ds(pl.multiple_of(n * 256, 256), 256)
        total = dot(xsh[...], tah[:, cols]) + dot(xsl[...], tah[:, cols]) + dot(xsh[...], tal[:, cols])
        other = dot(xdh[...], tbh[:, cols]) + dot(xdl[...], tbh[:, cols]) + dot(xdh[...], tbl[:, cols])
        for side, value in ((0, -(total + other)), (1, other - total)):
            where = pl.ds(pl.multiple_of(side * HALF + n * 256, 256), 256)
            along = flow[2, :, where]
            for i in range(3):
                slope = along * value[i * ROWS:(i + 1) * ROWS]
                if i == 2:
                    slope = slope + value[3 * ROWS:]
                pre[i, :, where] = flow[i, :, where] - 0.1 * slope
            div[:, where] = value[2 * ROWS:3 * ROWS]
        return carry
    lax.fori_loop(0, 3, slopes, 0)

    def places(s, carry):
        row = cells[pl.ds(s, 1), :] & (SPLIT - 1)
        def part(b, inner):
            index = lax.broadcasted_iota(jnp.int32, (16, MK), 0) + b * 16
            hot[s, pl.ds(pl.multiple_of(b * 16, 16), 16), :] = jnp.where(index == row, 1.0, 0.0).astype(BF16)
            return inner
        lax.fori_loop(0, SPLIT // 16, part, 0)
        return carry
    lax.fori_loop(0, ST, places, 0)

    square = lax.broadcasted_iota(jnp.int32, (ROWS, ROWS), 0) == lax.broadcasted_iota(jnp.int32, (ROWS, ROWS), 1)
    for zt in range(12):
        open_cells = jnp.where(square, 1.0 - solid[zt].astype(F32), 0.0).astype(BF16)
        fluid[:, pl.ds(zt * LANES, LANES)] = dot(open_cells, jnp.ones((ROWS, LANES), BF16))

    upper, scale = elimination()
    for group, (first, size) in enumerate(GROUPS):
        arrived(grp_block(grecv, pl.ds(0, NG - 1), group), 2 + group)

        def lines(t, carry):
            rows = pl.ds(pl.multiple_of(lax.div(t, size) * 8, 8), 8)
            cols = pl.ds(pl.multiple_of((first + lax.rem(t, size)) * LANES, LANES), LANES)
            f = [grecv[i, rows, cols] for i in range(NG)]
            get = lambda i: f[i] if 0 <= i < NG else jnp.zeros_like(f[0])
            done = []
            for i in range(NG):
                value = (7.0 / 9.0) * (get(i + 1) - get(i - 1)) + (1.0 / 36.0) * (get(i + 2) - get(i - 2))
                if i:
                    value = (value - done[-1] * (1.0 / 3.0)) * scale[i]
                done.append(value)
            value = done[-1]
            gmid[NG - 1, rows, cols] = value
            for i in reversed(range(NG - 1)):
                value = done[i] - upper[i] * value
                gmid[i, rows, cols] = value
            return carry
        lax.fori_loop(0, ROWS // 8 * size, lines, 0)

        arrived(pen_block(precv, pl.ds(0, NP - 1), group), group)
        for c in range(first, first + size):
            def halves(q, carry):
                rows = pl.ds(pl.multiple_of(q * ROWS, 16), ROWS)
                one, two = precv[q, c], precv[q + NP // 2, c]
                for both, packed in ((fsum, one + two), (fdif, one - two)):
                    value = jnp.concatenate([packed, swap(packed)], axis=0)
                    high = value.astype(BF16).astype(F32)
                    both[rows, :] = jnp.where(wide < LANES // 2, high, swap(value - high)).astype(BF16)
                return carry
            lax.fori_loop(0, NP // 2, halves, 0)

            def across(m, carry):
                rows = pl.ds(pl.multiple_of(m * 256, 256), 256)
                for out, high, low, both in ((ysum, tah, tal, fsum), (ydif, tbh, tbl, fdif)):
                    value = dot(high[rows, :], both[...])
                    out[rows, :] = value + swap(value) + dot(low[rows, :], both[...])
                return carry
            lax.fori_loop(0, 3, across, 0)

            def pieces(q, carry):
                rows = pl.ds(pl.multiple_of(q * ROWS, 8), ROWS)
                total, other = ysum[rows, :], ydif[rows, :]
                for slot, value in ((q, total + other), (q + NP // 2, total - other)):
                    pmid[slot, c] = jnp.where(lane, value[:24], swap(value[24:]))
                return carry
            lax.fori_loop(0, NP // 2, pieces, 0)
        exchange(
            lambda peer: push("pen", peer, pen_block(pmid, peer, group), pen_block(pback, me_p, group), 4 + group),
            lambda peer: push("grp", peer, grp_block(gmid, peer, group), grp_block(gback, me_g, group), 6 + group),
        )
        cols = pl.ds(first * LANES, size * LANES)
        gback[me_g, :, cols] = gmid[me_g, :, cols]
        for c in range(first, first + size):
            pback[me_p, c] = pmid[me_p, c]

    count = 3 * lax.broadcasted_iota(jnp.int32, (ROWS, MK), 0)
    acc[...] = jnp.zeros_like(acc)
    corr[...] = jnp.zeros_like(corr)
    for c in range(PARTS):
        for group, (first, size) in enumerate(GROUPS):
            if c == first:
                arrived(grp_block(gback, pl.ds(0, NG - 1), group), 6 + group)
                arrived(pen_block(pback, pl.ds(0, NP - 1), group), 4 + group)
        for k in range(4):
            cols = pl.ds((4 * c + k) * LANES, LANES)
            first, size = next(g for g in GROUPS if g[0] <= c < sum(g))
            at, lag = divmod(4 * (c - first) + k, size)
            d0 = [gback[4 * f + at, :, pl.ds((first + lag) * LANES, LANES)] for f in range(4)]
            d1 = []
            for f in range(4):
                one, two = pback[8 * f + 2 * k, c], pback[8 * f + 2 * k + 1, c]
                d1.append(jnp.concatenate([jnp.where(lane, one, swap(two)), jnp.where(lane, swap(one), two)], axis=0))
            u0, u1 = flow[0, :, cols], flow[1, :, cols]
            for i in range(3):
                slope = u0 * d0[i] + u1 * d1[i]
                if i == 0:
                    slope = slope + d0[3]
                if i == 1:
                    slope = slope + d1[3]
                value = pre[i, :, cols] - 0.1 * slope
                prov[i, :, cols] = value
                rows = pl.ds((3 * c + i) * ROWS, ROWS)
                phi[rows, pl.ds(k * LANES, LANES)], plo[rows, pl.ds(k * LANES, LANES)] = bf16_parts(value)
            div[:, cols] = div[:, cols] + d0[0] + d1[1]

        if c == PARTS - 1:
            for g in range(NG):
                tile, off = divmod(96 * g, LANES)
                value = div[:, pl.ds(tile * LANES, LANES)]
                if off:
                    value = pltpu.roll(value, LANES - off, 1)
                if off > 32:
                    rest = pltpu.roll(div[:, pl.ds((tile + 1) * LANES, LANES)], LANES - off, 1)
                    value = jnp.where(wide < LANES - off, value, rest)
                dsend[g] = value

            def spread_out(t, carry):
                peer = grp_peer(t)
                push("grp", peer, dsend.at[peer], drecv.at[me_g], 8)
                return carry
            lax.fori_loop(0, NG - 1, spread_out, 0)
            drecv[me_g] = dsend[me_g]

        def sample(s, carry):
            place = hot[s]
            rows = pl.ds(3 * c * ROWS, 3 * ROWS)
            got = dot(phi[rows, :], place) + dot(plo[rows, :], place)
            mask = count + c == cells[pl.ds(s, 1), :] >> 9
            weight = weights[pl.ds(s, 1), :]
            for i in range(3):
                picked = jnp.where(mask, got[i * ROWS:(i + 1) * ROWS], 0.0)
                acc[i] += jnp.sum(picked.reshape(6, 8, MK), axis=0) * weight
            return carry
        lax.fori_loop(0, ST, sample, 0)

    sampled = [jnp.sum(acc[i], axis=0, keepdims=True) for i in range(3)]

    def spread(s, carry):
        place = hot[s]
        code = cells[pl.ds(s, 1), :] >> 9
        weight = weights[pl.ds(s, 1), :]
        masks = [count + zb == code for zb in range(3)]
        parts = []
        for i in range(3):
            value = sampled[i] * weight
            high = value.astype(BF16).astype(F32)
            parts.append((high, (value - high).astype(BF16).astype(F32)))
        total = None
        for side in range(2):
            table = jnp.concatenate(
                [jnp.where(masks[zb], parts[i][side], 0.0).astype(BF16) for zb in range(3) for i in range(3)], axis=0
            )
            value = lax.dot_general(table, place, (((1,), (1,)), ((), ())), preferred_element_type=F32)
            total = value if total is None else total + value
        corr[...] += total
        return carry
    lax.fori_loop(0, ST, spread, 0)

    for zt in range(12):
        cols = pl.ds(zt * LANES, LANES)
        for i in range(3):
            part = corr[pl.ds((zt // 4 * 3 + i) * ROWS, ROWS), pl.ds(zt % 4 * LANES, LANES)]
            vel[i, :, cols] = fluid[:, cols] * (prov[i, :, cols] - part)

    arrived(drecv.at[pl.ds(0, NG - 1)], 8)
    pois[...] = drecv[:, :, :96]

    for group in range(len(GROUPS)):
        sent(pen_block(psend, pl.ds(0, NP - 1), group), group)
        sent(grp_block(grecv, pl.ds(0, NG - 1), group), 2 + group)
        sent(pen_block(pmid, pl.ds(0, NP - 1), group), 4 + group)
        sent(grp_block(gmid, pl.ds(0, NG - 1), group), 6 + group)
    sent(dsend.at[pl.ds(0, NG - 1)], 8)


def body(flow_fields, marker_cells, marker_weights, solid_blocks):
    vmem = pl.BlockSpec(memory_space=pltpu.VMEM)
    tables = [jnp.asarray(rows) for rows in table_rows()]
    V = pltpu.VMEM
    velocity, source = pl.pallas_call(
        kernel,
        name="substep",
        out_shape=(
            pltpu.VMEM((3, ROWS, NZ), F32),
            pltpu.VMEM((NG, ROWS, 96), F32),
        ),
        in_specs=[pl.BlockSpec(memory_space=pl.ANY)] + [vmem] * 7,
        out_specs=(vmem, vmem),
        scratch_shapes=[
            V((4, ROWS, NZ), F32),
            *[V((NP, PARTS, ROWS // 2, LANES), F32)] * 4,
            *[V((NG, ROWS, PARTS * LANES), F32)] * 3,
            V((NG, ROWS, LANES), F32), V((NG, ROWS, LANES), F32),
            V((HALF, HALF), BF16), V((HALF, HALF), BF16), V((HALF, HALF), BF16), V((HALF, HALF), BF16),
            V((4 * ROWS, HALF), BF16), V((4 * ROWS, HALF), BF16), V((4 * ROWS, HALF), BF16), V((4 * ROWS, HALF), BF16),
            V((HALF, LANES), F32), V((HALF, LANES), F32), V((HALF, LANES), BF16), V((HALF, LANES), BF16),
            V((3, ROWS, NZ), F32), V((ROWS, NZ), F32), V((3, ROWS, NZ), F32),
            V((9 * ROWS, SPLIT), BF16), V((9 * ROWS, SPLIT), BF16),
            V((ST, SPLIT, MK), BF16), V((9 * ROWS, SPLIT), F32), V((3, 8, MK), F32), V((ROWS, NZ), F32),
            pltpu.SemaphoreType.DMA((9,)), pltpu.SemaphoreType.DMA((9,)),
            pltpu.SemaphoreType.DMA,
        ],
        compiler_params=pltpu.CompilerParams(
            collective_id=0, has_side_effects=True, vmem_limit_bytes=60 * 1024 * 1024
        ),
    )(
        flow_fields.reshape(4, ROWS, NZ),
        marker_cells[0, 0].T,
        marker_weights[0, 0].T,
        solid_blocks.transpose(2, 0, 1),
        *tables,
    )
    return velocity.reshape(3, 1, ROWS, NZ), source


def solution(mesh):
    return jax.shard_map(
        body,
        mesh=mesh,
        in_specs=(
            P(None, "grp", "pen", None),
            P("grp", "pen", None, None),
            P("grp", "pen", None, None),
            P("grp", "pen", None),
        ),
        out_specs=(P(None, "grp", "pen", None), P(None, "pen", "grp")),
        check_vma=False,
    )
```

```python
import math

import jax
import jax.numpy as jnp
import numpy as np
from jax import lax
from jax.experimental import pallas as pl
from jax.experimental.pallas import tpu as pltpu
from jax.sharding import PartitionSpec as P

MESH = pl.DeviceIdType.MESH
F32, BF16 = jnp.float32, jnp.bfloat16
NG, NP = 16, 32
ROWS, NZ, HALF = 48, 1536, 768
LANES, SPLIT, MK, ST = 128, 512, 1024, 8
PARTS = NZ // SPLIT


def bf16_parts(values):
    high = values.astype(BF16)
    return high, (values - high.astype(F32)).astype(BF16)


def table_rows():
    lag = np.arange(2 * HALF)
    safe = np.where(lag % HALF == 0, 1, lag)
    line = math.pi / NZ * (1 - 2 * (lag % 2)) / np.tan(math.pi * safe / NZ)
    line = np.where(lag % HALF == 0, 0.0, line)
    other = np.roll(line, -HALF)
    rows = []
    for values, width in ((0.5 * (line + other), HALF), (0.5 * (line - other), 2 * HALF)):
        where = (np.arange(16)[:, None] - np.arange(width)[None, :]) % (2 * HALF)
        block = values[where].astype(np.float32)
        high = block.astype(jnp.bfloat16).astype(np.float32)
        rows += [high, (block - high).astype(jnp.bfloat16).astype(np.float32)]
    return rows


def elimination():
    upper, scale, last = [], [], 0.0
    for _ in range(NG):
        pivot = 1.0 / (1.0 - last / 3.0)
        last = pivot / 3.0
        upper.append(last)
        scale.append(pivot)
    return upper, scale


def kernel(
    source, cells, weights, solid, rah, ral, rbh, rbl,
    vel, pois,
    flow, psend, precv, pmid, pback, grecv, gmid, gback, dsend, drecv,
    tah, tal, tbh, tbl, xsh, xsl, xdh, xdl, ysum, ydif, fsum, fdif,
    pre, div, prov, phi, plo, hot, corr, acc, fluid,
    ssem, rsem, fsem,
):
    me_g, me_p = lax.axis_index("grp"), lax.axis_index("pen")
    lane = lax.broadcasted_iota(jnp.int32, (ROWS // 2, LANES), 1) < LANES // 2
    wide = lax.broadcasted_iota(jnp.int32, (ROWS, LANES), 1)
    dot = lambda a, b: jnp.dot(a, b, preferred_element_type=F32)
    swap = lambda value: pltpu.roll(value, LANES // 2, 1)
    barrier = pltpu.get_barrier_semaphore()

    def nth(k, middle, size):
        return lax.rem(middle + (1 - 2 * lax.rem(k, 2)) * lax.div(k + 1, 2), size)

    def pen_peer(t):
        z = lax.rem(lax.div(me_p, 2) + nth(lax.div(t, 4), 4, 8), 8)
        y = lax.rem(lax.div(me_p, 16) + 1 + lax.div(t, 2), 2)
        return y * 16 + z * 2 + lax.rem(me_p + t, 2)

    def grp_peer(t):
        x = lax.rem(me_g + nth(lax.div(t, 4), 2, 4), 4)
        y = lax.rem(lax.div(me_g, 4) + nth(lax.rem(t, 4), 2, 4), 4)
        return y * 4 + x

    def greet(axis, me, count):
        def step(d, carry):
            pl.semaphore_signal(
                barrier, 1, device_id={axis: lax.rem(me + d, count)}, device_id_type=MESH
            )
            return carry
        lax.fori_loop(1, count, step, 0)

    def push(axis, peer, src, dst, phase):
        pltpu.make_async_remote_copy(
            src_ref=src, dst_ref=dst, send_sem=ssem.at[phase], recv_sem=rsem.at[phase],
            device_id={axis: peer}, device_id_type=MESH,
        ).start()

    def exchange(to_pen, to_grp):
        def step(t, carry):
            to_pen(pen_peer(2 * t))
            to_pen(pen_peer(2 * t + 1))
            to_grp(grp_peer(t))
            return carry
        lax.fori_loop(0, NG - 1, step, 0)
        to_pen(pen_peer(NP - 1))

    def arrived(target, count, phase):
        ref = target.at[pl.ds(0, count - 1)]
        pltpu.make_async_copy(ref, ref, rsem.at[phase]).wait()

    def sent(source, count, phase):
        ref = source.at[pl.ds(0, count - 1)]
        pltpu.make_async_copy(ref, ref, ssem.at[phase]).wait()

    def mine(c, i):
        return flow.at[lax.div(i, 4), :, pl.ds(pl.multiple_of((lax.rem(i, 4) + 4 * c) * LANES, LANES), LANES)]

    fetch = pltpu.make_async_copy(source, flow, fsem)
    fetch.start()
    greet("pen", me_p, NP)
    greet("grp", me_g, NG)
    fetch.wait()

    for c in range(PARTS):
        for tile in range(16):
            cols = pl.ds((4 * c + tile % 4) * LANES, LANES)
            top, low = flow[tile // 4, :24, cols], flow[tile // 4, 24:, cols]
            psend[c, 2 * tile] = jnp.where(lane, top, swap(low))
            psend[c, 2 * tile + 1] = jnp.where(lane, swap(top), low)

    pl.semaphore_wait(barrier, NP - 1 + NG - 1)
    for c in range(PARTS):
        exchange(
            lambda peer: push("pen", peer, psend.at[c, peer], precv.at[c, me_p], c),
            lambda peer: push("grp", peer, mine(c, peer), grecv.at[c, me_g], PARTS + c),
        )
    for c in range(PARTS):
        precv[c, me_p] = psend[c, me_p]
        grecv[c, me_g] = mine(c, me_g)[...]

    def fill(b, carry):
        rows = pl.ds(pl.multiple_of(b * 16, 16), 16)
        tah[rows, :] = pltpu.roll(rah[...], b * 16, 1).astype(BF16)
        tal[rows, :] = pltpu.roll(ral[...], b * 16, 1).astype(BF16)
        tbh[rows, :] = pltpu.roll(rbh[...], b * 16, 1)[:, :HALF].astype(BF16)
        tbl[rows, :] = pltpu.roll(rbl[...], b * 16, 1)[:, :HALF].astype(BF16)
        return carry
    lax.fori_loop(0, HALF // 16, fill, 0)

    for f in range(4):
        rows = pl.ds(f * ROWS, ROWS)
        one, two = flow[f, :, :HALF], flow[f, :, HALF:]
        xsh[rows, :], xsl[rows, :] = bf16_parts(one + two)
        xdh[rows, :], xdl[rows, :] = bf16_parts(one - two)

    def slopes(n, carry):
        cols = pl.ds(pl.multiple_of(n * 256, 256), 256)
        total = dot(xsh[...], tah[:, cols]) + dot(xsl[...], tah[:, cols]) + dot(xsh[...], tal[:, cols])
        other = dot(xdh[...], tbh[:, cols]) + dot(xdl[...], tbh[:, cols]) + dot(xdh[...], tbl[:, cols])
        for side, value in ((0, -(total + other)), (1, other - total)):
            where = pl.ds(pl.multiple_of(side * HALF + n * 256, 256), 256)
            along = flow[2, :, where]
            for i in range(3):
                slope = along * value[i * ROWS:(i + 1) * ROWS]
                if i == 2:
                    slope = slope + value[3 * ROWS:]
                pre[i, :, where] = flow[i, :, where] - 0.1 * slope
            div[:, where] = value[2 * ROWS:3 * ROWS]
        return carry
    lax.fori_loop(0, 3, slopes, 0)

    def places(s, carry):
        row = cells[pl.ds(s, 1), :] & (SPLIT - 1)
        def part(b, inner):
            index = lax.broadcasted_iota(jnp.int32, (16, MK), 0) + b * 16
            hot[s, pl.ds(pl.multiple_of(b * 16, 16), 16), :] = jnp.where(index == row, 1.0, 0.0).astype(BF16)
            return inner
        lax.fori_loop(0, SPLIT // 16, part, 0)
        return carry
    lax.fori_loop(0, ST, places, 0)

    square = lax.broadcasted_iota(jnp.int32, (ROWS, ROWS), 0) == lax.broadcasted_iota(jnp.int32, (ROWS, ROWS), 1)
    for zt in range(12):
        open_cells = jnp.where(square, 1.0 - solid[zt].astype(F32), 0.0).astype(BF16)
        fluid[:, pl.ds(zt * LANES, LANES)] = dot(open_cells, jnp.ones((ROWS, LANES), BF16))

    upper, scale = elimination()
    for c in range(PARTS):
        arrived(grecv.at[c], NG, PARTS + c)

        def lines(t, carry):
            rows = pl.ds(pl.multiple_of(t * 8, 8), 8)
            f = [grecv[c, i, rows, :] for i in range(NG)]
            get = lambda i: f[i] if 0 <= i < NG else jnp.zeros_like(f[0])
            done = []
            for i in range(NG):
                value = (7.0 / 9.0) * (get(i + 1) - get(i - 1)) + (1.0 / 36.0) * (get(i + 2) - get(i - 2))
                if i:
                    value = (value - done[-1] * (1.0 / 3.0)) * scale[i]
                done.append(value)
            value = done[-1]
            gmid[c, NG - 1, rows, :] = value
            for i in reversed(range(NG - 1)):
                value = done[i] - upper[i] * value
                gmid[c, i, rows, :] = value
            return carry
        lax.fori_loop(0, ROWS // 8, lines, 0)
        gback[c, me_g] = gmid[c, me_g]

        arrived(precv.at[c], NP, c)

        def halves(q, carry):
            rows = pl.ds(pl.multiple_of(q * ROWS, 16), ROWS)
            one, two = precv[c, q], precv[c, q + NP // 2]
            for both, packed in ((fsum, one + two), (fdif, one - two)):
                value = jnp.concatenate([packed, swap(packed)], axis=0)
                high = value.astype(BF16).astype(F32)
                both[rows, :] = jnp.where(wide < LANES // 2, high, swap(value - high)).astype(BF16)
            return carry
        lax.fori_loop(0, NP // 2, halves, 0)

        def across(m, carry):
            rows = pl.ds(pl.multiple_of(m * 256, 256), 256)
            for out, high, low, both in ((ysum, tah, tal, fsum), (ydif, tbh, tbl, fdif)):
                value = dot(high[rows, :], both[...])
                out[rows, :] = value + swap(value) + dot(low[rows, :], both[...])
            return carry
        lax.fori_loop(0, 3, across, 0)

        def pieces(q, carry):
            rows = pl.ds(pl.multiple_of(q * ROWS, 8), ROWS)
            total, other = ysum[rows, :], ydif[rows, :]
            for slot, value in ((q, total + other), (q + NP // 2, total - other)):
                pmid[c, slot] = jnp.where(lane, value[:24], swap(value[24:]))
            return carry
        lax.fori_loop(0, NP // 2, pieces, 0)
        exchange(
            lambda peer: push("pen", peer, pmid.at[c, peer], pback.at[c, me_p], 2 * PARTS + c),
            lambda peer: push("grp", peer, gmid.at[c, peer], gback.at[c, me_g], 3 * PARTS + c),
        )
        pback[c, me_p] = pmid[c, me_p]

    count = 3 * lax.broadcasted_iota(jnp.int32, (ROWS, MK), 0)
    acc[...] = jnp.zeros_like(acc)
    corr[...] = jnp.zeros_like(corr)
    for c in range(PARTS):
        arrived(gback.at[c], NG, 3 * PARTS + c)
        arrived(pback.at[c], NP, 2 * PARTS + c)
        for k in range(4):
            cols = pl.ds((4 * c + k) * LANES, LANES)
            d0 = [gback[c, 4 * f + k] for f in range(4)]
            d1 = []
            for f in range(4):
                one, two = pback[c, 8 * f + 2 * k], pback[c, 8 * f + 2 * k + 1]
                d1.append(jnp.concatenate([jnp.where(lane, one, swap(two)), jnp.where(lane, swap(one), two)], axis=0))
            u0, u1 = flow[0, :, cols], flow[1, :, cols]
            for i in range(3):
                slope = u0 * d0[i] + u1 * d1[i]
                if i == 0:
                    slope = slope + d0[3]
                if i == 1:
                    slope = slope + d1[3]
                value = pre[i, :, cols] - 0.1 * slope
                prov[i, :, cols] = value
                rows = pl.ds((3 * c + i) * ROWS, ROWS)
                phi[rows, pl.ds(k * LANES, LANES)], plo[rows, pl.ds(k * LANES, LANES)] = bf16_parts(value)
            div[:, cols] = div[:, cols] + d0[0] + d1[1]

        if c == PARTS - 1:
            for g in range(NG):
                tile, off = divmod(96 * g, LANES)
                value = div[:, pl.ds(tile * LANES, LANES)]
                if off:
                    value = pltpu.roll(value, LANES - off, 1)
                if off > 32:
                    rest = pltpu.roll(div[:, pl.ds((tile + 1) * LANES, LANES)], LANES - off, 1)
                    value = jnp.where(wide < LANES - off, value, rest)
                dsend[g] = value

            def spread_out(t, carry):
                peer = grp_peer(t)
                push("grp", peer, dsend.at[peer], drecv.at[me_g], 4 * PARTS)
                return carry
            lax.fori_loop(0, NG - 1, spread_out, 0)
            drecv[me_g] = dsend[me_g]

        def sample(s, carry):
            place = hot[s]
            rows = pl.ds(3 * c * ROWS, 3 * ROWS)
            got = dot(phi[rows, :], place) + dot(plo[rows, :], place)
            mask = count + c == cells[pl.ds(s, 1), :] >> 9
            weight = weights[pl.ds(s, 1), :]
            for i in range(3):
                picked = jnp.where(mask, got[i * ROWS:(i + 1) * ROWS], 0.0)
                acc[i] += jnp.sum(picked.reshape(6, 8, MK), axis=0) * weight
            return carry
        lax.fori_loop(0, ST, sample, 0, unroll=8)

    sampled = [jnp.sum(acc[i], axis=0, keepdims=True) for i in range(3)]

    def spread(s, carry):
        place = hot[s]
        code = cells[pl.ds(s, 1), :] >> 9
        weight = weights[pl.ds(s, 1), :]
        masks = [count + zb == code for zb in range(3)]
        parts = []
        for i in range(3):
            value = sampled[i] * weight
            high = value.astype(BF16).astype(F32)
            parts.append((high, (value - high).astype(BF16).astype(F32)))
        total = None
        for side in range(2):
            table = jnp.concatenate(
                [jnp.where(masks[zb], parts[i][side], 0.0).astype(BF16) for zb in range(3) for i in range(3)], axis=0
            )
            value = lax.dot_general(table, place, (((1,), (1,)), ((), ())), preferred_element_type=F32)
            total = value if total is None else total + value
        corr[...] += total
        return carry
    lax.fori_loop(0, ST, spread, 0, unroll=2)

    for zt in range(12):
        cols = pl.ds(zt * LANES, LANES)
        for i in range(3):
            part = corr[pl.ds((zt // 4 * 3 + i) * ROWS, ROWS), pl.ds(zt % 4 * LANES, LANES)]
            vel[i, :, cols] = fluid[:, cols] * (prov[i, :, cols] - part)

    arrived(drecv, NG, 4 * PARTS)
    pois[...] = drecv[:, :, :96]

    for c in range(PARTS):
        sent(psend.at[c], NP, c)
        sent(grecv.at[c], NG, PARTS + c)
        sent(pmid.at[c], NP, 2 * PARTS + c)
        sent(gmid.at[c], NG, 3 * PARTS + c)
    sent(dsend, NG, 4 * PARTS)


def body(flow_fields, marker_cells, marker_weights, solid_blocks):
    vmem = pl.BlockSpec(memory_space=pltpu.VMEM)
    tables = [jnp.asarray(rows) for rows in table_rows()]
    V = pltpu.VMEM
    velocity, source = pl.pallas_call(
        kernel,
        name="substep",
        out_shape=(
            pltpu.VMEM((3, ROWS, NZ), F32),
            pltpu.VMEM((NG, ROWS, 96), F32),
        ),
        in_specs=[pl.BlockSpec(memory_space=pl.ANY)] + [vmem] * 7,
        out_specs=(vmem, vmem),
        scratch_shapes=[
            V((4, ROWS, NZ), F32),
            *[V((PARTS, NP, ROWS // 2, LANES), F32)] * 4,
            *[V((PARTS, NG, ROWS, LANES), F32)] * 3,
            V((NG, ROWS, LANES), F32), V((NG, ROWS, LANES), F32),
            V((HALF, HALF), BF16), V((HALF, HALF), BF16), V((HALF, HALF), BF16), V((HALF, HALF), BF16),
            V((4 * ROWS, HALF), BF16), V((4 * ROWS, HALF), BF16), V((4 * ROWS, HALF), BF16), V((4 * ROWS, HALF), BF16),
            V((HALF, LANES), F32), V((HALF, LANES), F32), V((HALF, LANES), BF16), V((HALF, LANES), BF16),
            V((3, ROWS, NZ), F32), V((ROWS, NZ), F32), V((3, ROWS, NZ), F32),
            V((9 * ROWS, SPLIT), BF16), V((9 * ROWS, SPLIT), BF16),
            V((ST, SPLIT, MK), BF16), V((9 * ROWS, SPLIT), F32), V((3, 8, MK), F32), V((ROWS, NZ), F32),
            pltpu.SemaphoreType.DMA((4 * PARTS + 1,)), pltpu.SemaphoreType.DMA((4 * PARTS + 1,)),
            pltpu.SemaphoreType.DMA,
        ],
        compiler_params=pltpu.CompilerParams(
            collective_id=0, has_side_effects=True, vmem_limit_bytes=60 * 1024 * 1024
        ),
    )(
        flow_fields.reshape(4, ROWS, NZ),
        marker_cells[0, 0].T,
        marker_weights[0, 0].T,
        solid_blocks.transpose(2, 0, 1),
        *tables,
    )
    return velocity.reshape(3, 1, ROWS, NZ), source


def solution(mesh):
    return jax.shard_map(
        body,
        mesh=mesh,
        in_specs=(
            P(None, "grp", "pen", None),
            P("grp", "pen", None, None),
            P("grp", "pen", None, None),
            P("grp", "pen", None),
        ),
        out_specs=(P(None, "grp", "pen", None), P(None, "pen", "grp")),
        check_vma=False,
    )
```
